32 devices in a mesh: row: 4 (over z), col: 2 (over x), depth: 4 (over y, core).
Axes of the slice: x: 2, y: 2, z: 4, core: 2. Of those that a mesh axis runs over, the one named last changes fastest.
Arguments:
- tokens: bfloat16 [2560, 8192], P(('row', 'depth'), 'col'), may hold values from -6 to 6
- weight: bfloat16 [8192, 4096], P('row', 'col'), may hold values from -0.0625 to 0.0625
- cotangent: bfloat16 [2560, 4096], P(('row', 'depth'), 'col'), may hold values from -6 to 6
- master: float32 [8192, 4096], P(('row', 'depth'), 'col'), may hold values from -0.1 to 0.1
- first_moment: float32 [8192, 4096], P(('row', 'depth'), 'col'), may hold values from -6 to 6
- second_moment: float32 [8192, 4096], P(('row', 'depth'), 'col'), may hold values from 0.1 to 10
Outputs:
- queries: bfloat16 [2560, 4096], P(('row', 'depth'), 'col')
- token_grad: bfloat16 [2560, 8192], P(('row', 'depth'), 'col')
- new_master: float32 [8192, 4096], P(('row', 'depth'), 'col')
- new_first: float32 [8192, 4096], P(('row', 'depth'), 'col')
- new_second: float32 [8192, 4096], P(('row', 'depth'), 'col')
- new_weight: bfloat16 [8192, 4096], P('row', 'col')
The draws below stay inside these ranges and needn't reach their ends.
All inputs are finite; a program needn't handle non-finite values.
Results may differ from the reference program's by a relative error of at most 0.001.
Values may be sent and summed in bfloat16 or wider, within the bound.
A program may use at most 128 MiB of HBM per device.

```python
import math
import jax
import jax.numpy as jnp

D = 8192
HQ = 4096
TOKENS = 2560


def strengthened(values, rng, source, target, blocks, factor):
    owner, partner = [(jnp.arange(values.shape[axis_at]) // (values.shape[axis_at] // blocks)).reshape([-1 if axis == axis_at else 1 for axis in range(values.ndim)]) for axis_at in (source, target)]
    chosen = jax.random.permutation(rng, blocks)[partner]
    strong = (owner == chosen) | (owner == (partner + blocks // 2) % blocks)
    return jnp.where(strong, factor * values, values)


def shard_levels(rng, dims, split, smallest, largest):
    def one(dim, blocks):
        heights = jax.random.uniform(jax.random.fold_in(jax.random.fold_in(rng, 6), dim), (blocks,), jnp.float32, smallest / len(split), largest / len(split))
        return jnp.repeat(jnp.exp(heights), dims[dim] // blocks).reshape((-1,) + (1,) * (len(dims) - dim - 1))

    gain = one(*split[0])
    for cut in split[1:]:
        gain = gain * one(*cut)
    return gain


def bell_draw(stream_key, dims, width, bound, shards=(), held_as=jnp.bfloat16):
    drawn = width * jax.random.normal(stream_key, dims, jnp.float32)
    if shards:
        drawn = drawn * shard_levels(stream_key, dims, shards, -0.22, 0.18)
    return jnp.clip(drawn, -bound, bound).astype(held_as)


def noise_with(key, shape, scale, reach, cuts, heavy, dtype=jnp.bfloat16):
    values = scale * jax.random.normal(key, shape, jnp.float32)
    if cuts:
        values = values * shard_levels(key, shape, cuts, -0.22, 0.18)
    return jnp.clip(strengthened(values, jax.random.fold_in(key, 3), *heavy), -reach, reach).astype(dtype)


def setup_inputs(seed: int = 0) -> dict:
    arg_keys = jax.random.split(jax.random.key(seed), 7)
    return {
        "tokens": noise_with(arg_keys[0], (TOKENS, D), 1.0, 6.0, ((0, 16), (1, 2)), (0, 1, 16, 2.0)),
        "weight": bell_draw(arg_keys[1], (D, HQ), D ** -0.5, 0.0625, ((0, 4), (1, 2))),
        "cotangent": bell_draw(arg_keys[2], (TOKENS, HQ), 1.0, 6.0, ((0, 16), (1, 2))),
        "master": jnp.clip(jax.random.uniform(arg_keys[3], (D, HQ), jnp.float32, -0.1, 0.1) * shard_levels(arg_keys[3], (D, HQ), ((0, 16), (1, 2)), -0.4, 0.0), -0.1, 0.1),
        "first_moment": bell_draw(arg_keys[4], (D, HQ), 1.0, 6.0, ((0, 16), (1, 2)), jnp.float32),
        "second_moment": jnp.clip(jnp.exp(math.log(10.0) - 4.6051702 * jax.random.uniform(arg_keys[5], (D, HQ), jnp.float32) ** shard_levels(arg_keys[5], (D, HQ), ((0, 16), (1, 2)), -0.2, 0.2)), 0.1, 10.0),
    }


beta_one = 0.9
beta_two = 0.95
learn_rate = 0.02
decay_rate = 0.1
adam_eps = 1e-08
bias_one = 1.0 - 0.9 ** 50
bias_two = 1.0 - 0.95 ** 50

def reference(tokens, weight, cotangent, master, first_moment, second_moment):
    queries = jnp.dot(tokens, weight, preferred_element_type=jnp.float32).astype(jnp.bfloat16)
    token_grad = jnp.dot(cotangent, weight.T, preferred_element_type=jnp.float32).astype(jnp.bfloat16)
    grad = jnp.dot(tokens.T, cotangent, preferred_element_type=jnp.float32) * (1.0 / math.sqrt(TOKENS))
    new_first = beta_one * first_moment + (1.0 - beta_one) * grad
    new_second = beta_two * second_moment + (1.0 - beta_two) * grad * grad
    step_value = new_first / bias_one / (jnp.sqrt(new_second / bias_two) + adam_eps)
    new_master = master - learn_rate * (step_value + decay_rate * master)
    new_weight = new_master.astype(jnp.bfloat16)
    return (queries, token_grad, new_master, new_first, new_second, new_weight)
```

```python
import math

import jax
import jax.numpy as jnp
from jax import lax
from jax.sharding import PartitionSpec as P

beta_one = 0.9
beta_two = 0.95
learn_rate = 0.02
decay_rate = 0.1
adam_eps = 1e-08
bias_one = 1.0 - 0.9**50
bias_two = 1.0 - 0.95**50


def local(tokens, weight, cotangent, master, first_moment, second_moment):
    rows, cols = lax.axis_size("row"), lax.axis_size("col")
    block = tokens.shape[0]
    total_tokens = block * rows * lax.axis_size("depth")
    grad_scale = 1.0 / math.sqrt(total_tokens)
    full_rows = lax.all_gather(tokens, "col", axis=1, tiled=True)
    line_cotangent = lax.all_gather(cotangent, "row", axis=0, tiled=True)
    line_tokens = lax.all_to_all(full_rows, "row", split_axis=1, concat_axis=0, tiled=True)
    partial_grad = lax.dot_general(
        line_cotangent, weight, (((1,), (1,)), ((), ())), preferred_element_type=jnp.float32
    )
    piece = lax.psum_scatter(partial_grad, "col", scatter_dimension=1, tiled=True).astype(
        jnp.bfloat16
    )
    partial_queries = jnp.dot(line_tokens, weight, preferred_element_type=jnp.float32)
    queries = lax.psum_scatter(partial_queries, "row", scatter_dimension=0, tiled=True).astype(
        jnp.bfloat16
    )
    piece = lax.all_to_all(
        piece.reshape(rows, block, -1), "row", split_axis=0, concat_axis=0, tiled=True
    )
    piece = lax.all_to_all(
        piece.reshape(cols, rows // cols, block, -1), "col", split_axis=0, concat_axis=0, tiled=True
    )
    token_grad = piece.transpose(2, 1, 0, 3).reshape(tokens.shape)
    token_slab = lax.all_to_all(line_tokens, "depth", split_axis=1, concat_axis=0, tiled=True)
    all_cotangent = lax.all_gather(line_cotangent, "depth", axis=0, tiled=True)
    product = lax.dot_general(
        token_slab,
        all_cotangent,
        (((0,), (0,)), ((), ())),
        preferred_element_type=jnp.float32,
    )
    grad = product * grad_scale
    new_first = beta_one * first_moment + (1.0 - beta_one) * grad
    new_second = beta_two * second_moment + (1.0 - beta_two) * grad * grad
    step_value = new_first / bias_one / (jnp.sqrt(new_second / bias_two) + adam_eps)
    new_master = master - learn_rate * (step_value + decay_rate * master)
    shard_weight = new_master.astype(jnp.bfloat16)
    new_weight = lax.all_gather(shard_weight, "depth", axis=0, tiled=True)
    return (queries, token_grad, new_master, new_first, new_second, new_weight)


def solution(mesh):
    in_specs = (
        P(("row", "depth"), "col"),
        P("row", "col"),
        P(("row", "depth"), "col"),
        P(("row", "depth"), "col"),
        P(("row", "depth"), "col"),
        P(("row", "depth"), "col"),
    )
    out_specs = (
        P(("row", "depth"), "col"),
        P(("row", "depth"), "col"),
        P(("row", "depth"), "col"),
        P(("row", "depth"), "col"),
        P(("row", "depth"), "col"),
        P("row", "col"),
    )
    return jax.shard_map(local, mesh=mesh, in_specs=in_specs, out_specs=out_specs, check_vma=False)
```

```python
import math

import jax
import jax.numpy as jnp
from jax import lax
from jax.sharding import PartitionSpec as P

beta_one = 0.9
beta_two = 0.95
learn_rate = 0.02
decay_rate = 0.1
adam_eps = 1e-08
bias_one = 1.0 - 0.9**50
bias_two = 1.0 - 0.95**50


def swap(value, axis, step):
    size = lax.axis_size(axis)
    return lax.ppermute(value, axis, [(i, i ^ step) for i in range(size)])


def spread(value, axis):
    pieces = [value]
    for step in range(1, lax.axis_size(axis)):
        top = 1 << (step.bit_length() - 1)
        low = step & -step
        pieces.append(swap(pieces[step - low], axis, low) if step != top else swap(value, axis, step))
    return pieces


def in_order(pieces, axis, dim):
    me = lax.axis_index(axis)
    size = pieces[0].shape[dim]
    shape = list(pieces[0].shape)
    shape[dim] = size * len(pieces)
    whole = jnp.zeros(shape, pieces[0].dtype)
    for step, piece in enumerate(pieces):
        whole = lax.dynamic_update_slice_in_dim(whole, piece, (me ^ step) * size, dim)
    return whole


def local(tokens, weight, cotangent, master, first_moment, second_moment):
    rows, cols, depths = lax.axis_size("row"), lax.axis_size("col"), lax.axis_size("depth")
    col_at, depth_at = lax.axis_index("col"), lax.axis_index("depth")
    block = tokens.shape[0]
    total_tokens = block * rows * depths
    grad_scale = 1.0 / math.sqrt(total_tokens)
    full_rows = in_order(spread(tokens, "col"), "col", 1)
    line_cotangent = lax.all_gather(cotangent, "row", axis=0, tiled=True)
    line_tokens = lax.all_to_all(full_rows, "row", split_axis=1, concat_axis=0, tiled=True)
    features = weight.shape[0] // cols
    parts = []
    for step in reversed(range(cols)):
        panel = lax.dynamic_slice_in_dim(weight, (col_at ^ step) * features, features, 0)
        part = lax.dot_general(
            line_cotangent, panel, (((1,), (1,)), ((), ())), preferred_element_type=jnp.float32
        )
        parts.append(swap(part, "col", step) if step else part)
    piece = sum(parts[1:], parts[0]).astype(jnp.bfloat16)
    partial_queries = jnp.dot(line_tokens, weight, preferred_element_type=jnp.float32)
    queries = lax.psum_scatter(partial_queries, "row", scatter_dimension=0, tiled=True).astype(
        jnp.bfloat16
    )
    piece = lax.all_to_all(
        piece.reshape(rows, block, -1), "row", split_axis=0, concat_axis=0, tiled=True
    )
    piece = lax.all_to_all(
        piece.reshape(cols, rows // cols, block, -1), "col", split_axis=0, concat_axis=0, tiled=True
    )
    token_grad = piece.transpose(2, 1, 0, 3).reshape(tokens.shape)
    shard = line_tokens.shape[1] // depths
    product = 0.0
    for step, other_cotangent in enumerate(spread(line_cotangent, "depth")):
        slab = lax.dynamic_slice_in_dim(line_tokens, (depth_at ^ step) * shard, shard, 1)
        slab = swap(slab, "depth", step) if step else slab
        product = product + lax.dot_general(
            slab, other_cotangent, (((0,), (0,)), ((), ())), preferred_element_type=jnp.float32
        )
    grad = product * grad_scale
    new_first = beta_one * first_moment + (1.0 - beta_one) * grad
    new_second = beta_two * second_moment + (1.0 - beta_two) * grad * grad
    step_value = new_first / bias_one / (jnp.sqrt(new_second / bias_two) + adam_eps)
    new_master = master - learn_rate * (step_value + decay_rate * master)
    shard_weight = new_master.astype(jnp.bfloat16)
    new_weight = in_order(spread(shard_weight, "depth"), "depth", 0)
    return (queries, token_grad, new_master, new_first, new_second, new_weight)


def solution(mesh):
    in_specs = (
        P(("row", "depth"), "col"),
        P("row", "col"),
        P(("row", "depth"), "col"),
        P(("row", "depth"), "col"),
        P(("row", "depth"), "col"),
        P(("row", "depth"), "col"),
    )
    out_specs = (
        P(("row", "depth"), "col"),
        P(("row", "depth"), "col"),
        P(("row", "depth"), "col"),
        P(("row", "depth"), "col"),
        P(("row", "depth"), "col"),
        P("row", "col"),
    )
    return jax.shard_map(local, mesh=mesh, in_specs=in_specs, out_specs=out_specs, check_vma=False)
```

```python
import math

import jax
import jax.numpy as jnp
from jax import lax
from jax.sharding import PartitionSpec as P


beta_one = 0.9
beta_two = 0.95
learn_rate = 0.02
decay_rate = 0.1
adam_eps = 1e-08
bias_one = 1.0 - 0.9**50
bias_two = 1.0 - 0.95**50


def swap(value, axis, step):
    size = lax.axis_size(axis)
    return lax.ppermute(value, axis, [(i, i ^ step) for i in range(size)])


def spread(value, axis):
    pieces = [value]
    for step in range(1, lax.axis_size(axis)):
        top = 1 << (step.bit_length() - 1)
        low = step & -step
        pieces.append(swap(pieces[step - low], axis, low) if step != top else swap(value, axis, step))
    return pieces


def exchange(value, axis, dim, width):
    me = lax.axis_index(axis)
    pieces = []
    for step in range(lax.axis_size(axis)):
        piece = lax.dynamic_slice_in_dim(value, (me ^ step) * width, width, dim)
        pieces.append(swap(piece, axis, step) if step else piece)
    return pieces


def in_order(pieces, axis, dim):
    me = lax.axis_index(axis)
    size = pieces[0].shape[dim]
    shape = list(pieces[0].shape)
    shape[dim] = size * len(pieces)
    whole = jnp.zeros(shape, pieces[0].dtype)
    for step, piece in enumerate(pieces):
        whole = lax.dynamic_update_slice_in_dim(whole, piece, (me ^ step) * size, dim)
    return whole


def step(tokens, weight, cotangent, master, first_moment, second_moment):
    rows, cols, depths = lax.axis_size("row"), lax.axis_size("col"), lax.axis_size("depth")
    col_at = lax.axis_index("col")
    block = tokens.shape[0]
    total_tokens = block * rows * depths
    grad_scale = 1.0 / math.sqrt(total_tokens)
    full_rows = in_order(spread(tokens, "col"), "col", 1)
    line_cotangent = lax.all_gather(cotangent, "row", axis=0, tiled=True)
    line_pieces = exchange(full_rows, "row", 1, weight.shape[0])
    features = weight.shape[0] // cols
    parts = []
    for step in reversed(range(cols)):
        panel = lax.dynamic_slice_in_dim(weight, (col_at ^ step) * features, features, 0)
        part = lax.dot_general(
            line_cotangent, panel, (((1,), (1,)), ((), ())), preferred_element_type=jnp.float32
        )
        parts.append(swap(part, "col", step) if step else part)
    piece = sum(parts[1:], parts[0]).astype(jnp.bfloat16)
    line_tokens = in_order(line_pieces, "row", 0)
    partial_queries = jnp.dot(line_tokens, weight, preferred_element_type=jnp.float32)
    queries = lax.psum_scatter(partial_queries, "row", scatter_dimension=0, tiled=True).astype(
        jnp.bfloat16
    )
    piece = in_order(exchange(piece, "row", 0, block), "row", 0)
    piece = in_order(exchange(piece, "col", 0, block * rows // cols), "col", 0)
    piece = piece.reshape(cols, rows // cols, block, -1)
    token_grad = piece.transpose(2, 1, 0, 3).reshape(tokens.shape)
    shard = line_tokens.shape[1] // depths
    product = 0.0
    slabs = exchange(line_tokens, "depth", 1, shard)
    cotangents = spread(line_cotangent, "depth")
    for slab, other_cotangent in zip(slabs, cotangents):
        product = product + lax.dot_general(
            slab, other_cotangent, (((0,), (0,)), ((), ())), preferred_element_type=jnp.float32
        )
    grad = product * grad_scale
    new_first = beta_one * first_moment + (1.0 - beta_one) * grad
    new_second = beta_two * second_moment + (1.0 - beta_two) * grad * grad
    step_value = new_first / bias_one / (jnp.sqrt(new_second / bias_two) + adam_eps)
    new_master = master - learn_rate * (step_value + decay_rate * master)
    shard_weight = new_master.astype(jnp.bfloat16)
    new_weight = in_order(spread(shard_weight, "depth"), "depth", 0)
    return (queries, token_grad, new_master, new_first, new_second, new_weight)


def solution(mesh):
    in_specs = (
        P(("row", "depth"), "col"),
        P("row", "col"),
        P(("row", "depth"), "col"),
        P(("row", "depth"), "col"),
        P(("row", "depth"), "col"),
        P(("row", "depth"), "col"),
    )
    out_specs = (
        P(("row", "depth"), "col"),
        P(("row", "depth"), "col"),
        P(("row", "depth"), "col"),
        P(("row", "depth"), "col"),
        P(("row", "depth"), "col"),
        P("row", "col"),
    )
    return jax.shard_map(step, mesh=mesh, in_specs=in_specs, out_specs=out_specs, check_vma=False)
```

```python
import math

import jax
import jax.numpy as jnp
from jax import lax
from jax.sharding import PartitionSpec as P


beta_one = 0.9
beta_two = 0.95
learn_rate = 0.02
decay_rate = 0.1
adam_eps = 1e-08
bias_one = 1.0 - 0.9**50
bias_two = 1.0 - 0.95**50


def swap(value, axis, step):
    size = lax.axis_size(axis)
    return lax.ppermute(value, axis, [(i, i ^ step) for i in range(size)])


def spread(value, axis):
    pieces = [value]
    for step in range(1, lax.axis_size(axis)):
        top = 1 << (step.bit_length() - 1)
        low = step & -step
        pieces.append(
            swap(value, axis, step) if step == top else swap(pieces[step - low], axis, low)
        )
    return pieces


def exchange(value, axis, dim, width):
    me = lax.axis_index(axis)
    pieces = []
    for step in range(lax.axis_size(axis)):
        piece = lax.dynamic_slice_in_dim(value, (me ^ step) * width, width, dim)
        pieces.append(swap(piece, axis, step) if step else piece)
    return pieces


def in_order(pieces, axis, dim):
    me = lax.axis_index(axis)
    size = pieces[0].shape[dim]
    shape = list(pieces[0].shape)
    shape[dim] = size * len(pieces)
    whole = jnp.zeros(shape, pieces[0].dtype)
    for step, piece in enumerate(pieces):
        whole = lax.dynamic_update_slice_in_dim(whole, piece, (me ^ step) * size, dim)
    return whole


def step(tokens, weight, cotangent, master, first_moment, second_moment):
    rows, cols, depths = lax.axis_size("row"), lax.axis_size("col"), lax.axis_size("depth")
    col_at = lax.axis_index("col")
    block = tokens.shape[0]
    total_tokens = block * rows * depths
    grad_scale = 1.0 / math.sqrt(total_tokens)
    full_rows = in_order(spread(tokens, "col"), "col", 1)
    line_cotangent = lax.all_gather(cotangent, "row", axis=0, tiled=True)
    line_pieces = exchange(full_rows, "row", 1, weight.shape[0])
    features = weight.shape[0] // cols
    parts = []
    for step in reversed(range(cols)):
        panel = lax.dynamic_slice_in_dim(weight, (col_at ^ step) * features, features, 0)
        part = lax.dot_general(
            line_cotangent, panel, (((1,), (1,)), ((), ())), preferred_element_type=jnp.float32
        )
        parts.append(swap(part, "col", step) if step else part)
    piece = sum(parts[1:], parts[0]).astype(jnp.bfloat16)
    line_tokens = in_order(line_pieces, "row", 0)
    partial_queries = jnp.dot(line_tokens, weight, preferred_element_type=jnp.float32)
    queries = lax.psum_scatter(partial_queries, "row", scatter_dimension=0, tiled=True).astype(
        jnp.bfloat16
    )
    piece = in_order(exchange(piece, "row", 0, block), "row", 0)
    piece = in_order(exchange(piece, "col", 0, block * rows // cols), "col", 0)
    piece = piece.reshape(cols, rows // cols, block, -1)
    token_grad = piece.transpose(2, 1, 0, 3).reshape(tokens.shape)
    shard = line_tokens.shape[1] // depths
    product = 0.0
    slabs = exchange(line_tokens, "depth", 1, shard)
    cotangents = spread(line_cotangent, "depth")
    for slab, other_cotangent in zip(slabs, cotangents):
        product = product + lax.dot_general(
            slab, other_cotangent, (((0,), (0,)), ((), ())), preferred_element_type=jnp.float32
        )
    grad = product * grad_scale
    new_first = beta_one * first_moment + (1.0 - beta_one) * grad
    new_second = beta_two * second_moment + (1.0 - beta_two) * grad * grad
    step_value = new_first / bias_one / (jnp.sqrt(new_second / bias_two) + adam_eps)
    new_master = master - learn_rate * (step_value + decay_rate * master)
    shard_weight = new_master.astype(jnp.bfloat16)
    weight_pieces = spread(shard_weight, "depth")
    new_weight = in_order(weight_pieces, "depth", 0)
    return (queries, token_grad, new_master, new_first, new_second, new_weight)


def solution(mesh):
    in_specs = (
        P(("row", "depth"), "col"),
        P("row", "col"),
        P(("row", "depth"), "col"),
        P(("row", "depth"), "col"),
        P(("row", "depth"), "col"),
        P(("row", "depth"), "col"),
    )
    out_specs = (
        P(("row", "depth"), "col"),
        P(("row", "depth"), "col"),
        P(("row", "depth"), "col"),
        P(("row", "depth"), "col"),
        P(("row", "depth"), "col"),
        P("row", "col"),
    )
    return jax.shard_map(step, mesh=mesh, in_specs=in_specs, out_specs=out_specs, check_vma=False)
```
